768 devices in a mesh: row: 32 (over y_lo, x, core), col: 24 (over y_hi, z).
Axes of the slice: x: 4, y: 8 (y_hi: 2, y_lo: 4; y = y_hi * 4 + y_lo), z: 12, core: 2. Of those that a mesh axis runs over, the one named last changes fastest.
Arguments:
- trial: float32 [1, 256, 1024], P(None, None, 'row'), may hold values from -6 to 6
- screened: bfloat16 [18432, 18432], P('row', 'col'), may hold values from -0.15625 to 0.15625
- val_points: bfloat16 [18432, 256], P('row'), may hold values from -0.375 to 0.375
- cond_points: bfloat16 [18432, 1024], P('col', 'row'), may hold values from -0.1875 to 0.1875
- eps_val: float32 [256], replicated, may hold values from -0.6 to -0.1
- eps_cond: float32 [1024], replicated, may hold values from 0.1 to 1
Outputs:
- applied: float32 [1, 256, 1024], P(None, None, 'row')
The draws below stay inside these ranges and needn't reach their ends.
All inputs are finite; a program needn't handle non-finite values.
Results may differ from the reference program's by a relative error of at most 0.02.
Values may be sent and summed in bfloat16 or wider, within the bound.
No kernel may reach another device: no remote copies, remote signals or barrier semaphores. Data moves between devices by JAX's collectives and lax.ppermute only.
A program may use at most 32 MiB of HBM per device.

```python
import jax
import jax.numpy as jnp
from jax import lax

NV = 256
NC = 1024
NB = 1
APPLY = 2
P_SIZE = 18432
N_ROW = 32
N_COL = 24


def block_levels(key, extent, pieces, least, top_value):
    gain = 1.0
    for dim, parts in pieces:
        steps = jax.random.uniform(jax.random.fold_in(jax.random.fold_in(key, 6), dim), (parts,), jnp.float32, least / len(pieces), top_value / len(pieces))
        gain = gain * jnp.repeat(jnp.exp(steps), extent[dim] // parts).reshape((-1,) + (1,) * (len(extent) - 1 - dim))
    return gain


def gaussian(rng, dims, width, bound, shards=(), held_as=jnp.bfloat16):
    drawn = jax.random.normal(rng, dims, jnp.float32) * width
    if len(shards) > 0:
        drawn = block_levels(rng, dims, shards, -0.22, 0.18) * drawn
    return jnp.clip(drawn, min=-bound, max=bound).astype(held_as)


def setup_inputs(seed: int = 0) -> dict:
    arg_keys = jax.random.split(jax.random.key(seed), 7)
    trial = gaussian(arg_keys[0], (NB, NV, NC), 1.0, 6.0, ((2, 32),), jnp.float32)
    screened = gaussian(arg_keys[1], (P_SIZE, P_SIZE), (P_SIZE * P_SIZE // (NV * NC)) ** -0.5, 0.15625, ((0, 32), (1, 24)))
    val_points = gaussian(arg_keys[2], (P_SIZE, NV), NV ** -0.5, 0.375, ((0, 32),))
    cond_points = gaussian(arg_keys[3], (P_SIZE, NC), NC ** -0.5, 0.1875, ((0, 24), (1, 32)))
    eps_val = jnp.clip(jax.random.uniform(arg_keys[4], (NV,), jnp.float32, -0.6, -0.1), -0.6, -0.1)
    eps_cond = jnp.clip(jax.random.uniform(arg_keys[5], (NC,), jnp.float32, 0.1, 1.0), 0.1, 1.0)
    return dict(trial=trial, screened=screened, val_points=val_points, cond_points=cond_points, eps_val=eps_val, eps_cond=eps_cond)


def reference(trial, screened, val_points, cond_points, eps_val, eps_cond):
    energy = eps_cond[None, :] - eps_val[:, None]
    block = P_SIZE // N_ROW
    cblock = P_SIZE // N_COL
    cond_wide = cond_points.astype(jnp.float32)
    val_wide = val_points.astype(jnp.float32)
    current = trial
    for step in range(APPLY):
        xb = current.astype(jnp.bfloat16)
        pair = jnp.einsum('mv,bvc->bmc', val_wide, xb.astype(jnp.float32)).astype(jnp.bfloat16)

        def one_block(total, index):
            start = (index * block).astype(jnp.int32)
            pair_blk = lax.dynamic_slice_in_dim(pair, start, block, 1).astype(jnp.float32)
            screen_blk = lax.dynamic_slice_in_dim(screened, start, block, 0).astype(jnp.float32)
            val_blk = lax.dynamic_slice_in_dim(val_wide, start, block, 0)
            inner = jnp.einsum('bmc,nc->bmn', pair_blk, cond_wide)
            tile = (screen_blk[None] * inner).astype(jnp.bfloat16)

            def one_column(acc, jindex):
                cstart = (jindex * cblock).astype(jnp.int32)
                tile_col = lax.dynamic_slice_in_dim(tile, cstart, cblock, 2).astype(jnp.float32)
                cond_col = lax.dynamic_slice_in_dim(cond_wide, cstart, cblock, 0)
                back = jnp.einsum('bmn,nc->bmc', tile_col, cond_col).astype(jnp.bfloat16)
                term = jnp.einsum('mv,bmc->bvc', val_blk, back.astype(jnp.float32)).astype(jnp.bfloat16)
                return acc + term.astype(jnp.float32), None

            total, _ = lax.scan(one_column, total, jnp.arange(N_COL, dtype=jnp.int32))
            return total, None

        kernel, _ = lax.scan(one_block, jnp.zeros((NB, NV, NC), jnp.float32), jnp.arange(N_ROW, dtype=jnp.int32))
        current = energy[None] * current + kernel
    return current
```

```python
import jax
import jax.numpy as jnp
from jax import lax
from jax.sharding import Mesh, PartitionSpec as P

APPLY = 2
F32 = jnp.float32
BF16 = jnp.bfloat16

YX = ("ylo", "x")
ROW = ("ylo", "x", "core")
COL = ("yhi", "z")


def copies_from_all(array, axes):
    devices = lax.axis_size(axes)
    copies = jnp.broadcast_to(array, (devices, *array.shape))
    return lax.all_to_all(copies, axes, 0, 0, tiled=True)


def summed_over_copies(array, axes):
    return jnp.sum(copies_from_all(array, axes).astype(F32), axis=0)


def summed_over_pair(array, axis):
    both = lax.all_gather(array, axis, axis=0, tiled=False)
    return both[0].astype(F32) + both[1].astype(F32)


def body(trial, screened, val_points, cond_points, eps_val, eps_cond):
    nv, width = trial.shape[1], trial.shape[2]
    n_cols = cond_points.shape[0]
    peers = lax.axis_size(YX)
    offset = lax.axis_index(ROW) * width
    energy = lax.dynamic_slice_in_dim(eps_cond, offset, width, 0)[:, None] - eps_val[None, :]

    x_mine = trial[0].T
    mine = jnp.concatenate([cond_points.T, x_mine.astype(BF16)], axis=1)
    everything = copies_from_all(mine, YX).reshape(peers * width, n_cols + nv)
    cond_half = everything[:, :n_cols]
    x_half = everything[:, n_cols:]

    for step in range(APPLY):
        mixed_part = jnp.einsum("cv,cn->vn", x_half, cond_half, preferred_element_type=F32)
        mixed = summed_over_pair(mixed_part.astype(BF16), "core").astype(BF16)
        inner = jnp.einsum("mv,vn->mn", val_points, mixed, preferred_element_type=F32)
        tile = (screened * inner).astype(BF16)
        folded_part = jnp.einsum("mv,mn->vn", val_points, tile, preferred_element_type=F32)
        folded = summed_over_pair(folded_part.astype(BF16), "core").astype(BF16)
        terms = jnp.einsum("cn,vn->cv", cond_half, folded, preferred_element_type=F32)
        terms = terms.astype(BF16).reshape(peers, width, nv)
        rows = jnp.sum(lax.all_to_all(terms, YX, 0, 0, tiled=True).astype(F32), axis=0)
        along_z = summed_over_copies(rows.astype(BF16), "z")
        kernel_mine = summed_over_pair(along_z.astype(BF16), "yhi")
        x_mine = energy * x_mine + kernel_mine
        if step + 1 < APPLY:
            x_half = copies_from_all(x_mine.astype(BF16), YX).reshape(peers * width, nv)
    return x_mine.T[None]


def solution(mesh):
    devices = mesh.devices.reshape(4, 4, 2, 2, 12)
    fine = Mesh(devices, ("ylo", "x", "core", "yhi", "z"))
    in_specs = (P(None, None, ROW), P(ROW, COL), P(ROW, None), P(COL, ROW), P(), P())
    out_specs = P(None, None, ROW)
    return jax.shard_map(body, mesh=fine, in_specs=in_specs, out_specs=out_specs, check_vma=False)
```

```python
import jax
import jax.numpy as jnp
from jax import lax
from jax.sharding import Mesh, PartitionSpec as P

APPLY = 2
F32 = jnp.float32
BF16 = jnp.bfloat16

ROW = ("y2", "y1", "x", "core")
COL = ("yhi", "z")
NEAR = ("y1", "x")
PLANE = ("y1", "x", "y2")
WIDE = ("y1", "x", "y2", "yhi")


def copies_from_all(array, axes):
    devices = lax.axis_size(axes)
    copies = jnp.broadcast_to(array, (devices, *array.shape))
    return lax.all_to_all(copies, axes, 0, 0, tiled=True)


def summed_over_copies(array, axes):
    return jnp.sum(copies_from_all(array, axes).astype(F32), axis=0)


def summed_over_pair(array, axis):
    both = lax.all_gather(array, axis, axis=0, tiled=False)
    return both[0].astype(F32) + both[1].astype(F32)


def sent_and_summed(blocks, axes):
    return jnp.sum(lax.all_to_all(blocks, axes, 0, 0, tiled=True).astype(F32), axis=0)


def rows_from(array, start, rows):
    return lax.dynamic_slice(array, (start, jnp.uint32(0)), (rows, array.shape[1]))


def body(trial, screened, val_points, cond_points, eps_val, eps_cond):
    nv, width = trial.shape[1], trial.shape[2]
    n_cols = cond_points.shape[0]
    blocks = lax.axis_size(PLANE)
    half = width // 2
    offset = lax.axis_index(ROW) * width
    energy = lax.dynamic_slice_in_dim(eps_cond, offset, width, 0)[:, None] - eps_val[None, :]

    x_mine = trial[0].T
    mine = jnp.concatenate([cond_points.T, x_mine.astype(BF16)], axis=1)
    piece = lax.convert_element_type(lax.axis_index("yhi") * half, jnp.uint32)
    own = lax.convert_element_type(lax.axis_index(PLANE) * width, jnp.uint32)
    mine, energy, piece, own = lax.optimization_barrier((mine, energy, piece, own))
    two = lax.all_gather(mine, "y2", axis=0, tiled=False)
    everything = copies_from_all(two, NEAR).reshape(blocks * width, n_cols + nv)
    cond_half = everything[:, :n_cols]
    x_half = everything[:, n_cols:]

    def terms_of(x_half):
        mixed_part = jnp.einsum("cv,cn->vn", x_half, cond_half, preferred_element_type=F32)
        mixed = summed_over_pair(mixed_part.astype(BF16), "core").astype(BF16)
        inner = jnp.einsum("mv,vn->mn", val_points, mixed, preferred_element_type=F32)
        tile = (screened * inner).astype(BF16)
        folded_part = jnp.einsum("mv,mn->vn", val_points, tile, preferred_element_type=F32)
        folded = summed_over_pair(folded_part.astype(BF16), "core").astype(BF16)
        terms = jnp.einsum("cn,vn->cv", cond_half, folded, preferred_element_type=F32)
        return terms.astype(BF16)

    x_piece = rows_from(x_mine, piece, half)
    energy_piece = rows_from(energy, piece, half)
    for _ in range(APPLY - 1):
        terms = terms_of(x_half).reshape(2 * blocks, half, nv)
        rows = sent_and_summed(terms, WIDE)
        x_piece = energy_piece * x_piece + summed_over_copies(rows.astype(BF16), "z")
        x_half = copies_from_all(x_piece.astype(BF16), WIDE).reshape(blocks * width, nv)

    terms = terms_of(x_half).reshape(blocks, 1, width, nv)
    twice = jnp.broadcast_to(terms, (blocks, 2, width, nv)).reshape(2 * blocks, width, nv)
    rows = sent_and_summed(twice, WIDE)
    x_mine = rows_from(x_half, own, width)
    x_mine = energy * x_mine.astype(F32) + summed_over_copies(rows.astype(BF16), "z")
    return x_mine.T[None]


def solution(mesh):
    devices = mesh.devices.reshape(2, 2, 4, 2, 2, 12)
    fine = Mesh(devices, ("y2", "y1", "x", "core", "yhi", "z"))
    in_specs = (P(None, None, ROW), P(ROW, COL), P(ROW, None), P(COL, ROW), P(), P())
    out_specs = P(None, None, ROW)
    return jax.shard_map(body, mesh=fine, in_specs=in_specs, out_specs=out_specs, check_vma=False)
```

```python
import jax
import jax.numpy as jnp
from jax import lax
from jax.experimental import pallas as pl
from jax.experimental.pallas import tpu as pltpu
from jax.sharding import Mesh, PartitionSpec as P

APPLY = 2
F32 = jnp.float32
BF16 = jnp.bfloat16

ROW = ("y2", "y1", "x", "core")
COL = ("yhi", "z")
NEAR = ("y1", "x")
PLANE = ("y1", "x", "y2")
WIDE = ("y1", "x", "y2", "yhi")

VMEM = pl.BlockSpec(memory_space=pltpu.VMEM)


def start_kernel(offset_ref, trial_ref, cond_ref, val_ref, levels_ref, mine_ref, energy_ref):
    width, n_cols = cond_ref.shape
    lanes = levels_ref.shape[1]
    mine_ref[:, :n_cols] = cond_ref[...]
    mine_ref[:, n_cols:] = trial_ref[...].astype(BF16)
    offset = offset_ref[0]
    group = levels_ref[pl.ds(offset // lanes, 1), :]
    lane = lax.broadcasted_iota(jnp.int32, (width, lanes), 1)
    row = lax.broadcasted_iota(jnp.int32, (width, lanes), 0)
    picked = jnp.where(lane == row + offset % lanes, group, 0.0)
    energy_ref[...] = jnp.sum(picked, axis=1, keepdims=True) - val_ref[...]


def start(offset, trial, cond, eps_val, eps_cond):
    width, n_cols = cond.shape
    nv = trial.shape[1]
    lanes = 128
    return pl.pallas_call(
        start_kernel,
        out_shape=(
            jax.ShapeDtypeStruct((width, n_cols + nv), BF16),
            jax.ShapeDtypeStruct((width, nv), F32),
        ),
        in_specs=[pl.BlockSpec(memory_space=pltpu.SMEM), VMEM, VMEM, VMEM, VMEM],
        out_specs=(VMEM, VMEM),
        compiler_params=pltpu.CompilerParams(vmem_limit_bytes=1 << 20),
        name="start",
    )(offset, trial, cond, eps_val.reshape(1, nv), eps_cond.reshape(-1, lanes))


def tile_kernel(both_ref, val_ref, screened_ref, out_ref, tile):
    nv = out_ref.shape[0]
    mixed = (both_ref[:nv, :].astype(F32) + both_ref[nv:, :].astype(F32)).astype(BF16)
    inner = jnp.dot(val_ref[...], mixed, preferred_element_type=F32)
    tile[...] = (screened_ref[...].astype(F32) * inner).astype(BF16)
    folded = lax.dot_general(val_ref[...], tile[...], (((0,), (0,)), ((), ())), preferred_element_type=F32)
    out_ref[...] = folded.astype(BF16)


def folded_tile(both, val_points, screened):
    m, nv = val_points.shape
    n = screened.shape[1]
    return pl.pallas_call(
        tile_kernel,
        out_shape=jax.ShapeDtypeStruct((nv, n), BF16),
        in_specs=[VMEM, VMEM, VMEM],
        out_specs=VMEM,
        scratch_shapes=[pltpu.VMEM((m, n), BF16)],
        compiler_params=pltpu.CompilerParams(vmem_limit_bytes=16 << 20),
        cost_estimate=pl.CostEstimate(flops=4 * m * n * nv, bytes_accessed=2 * m * n, transcendentals=0),
        name="tile",
    )(both.reshape(2 * nv, n), val_points, screened)


def copies_from_all(array, axes):
    devices = lax.axis_size(axes)
    copies = jnp.broadcast_to(array, (devices, *array.shape))
    return lax.all_to_all(copies, axes, 0, 0, tiled=True)


def summed_over_copies(array, axes):
    return jnp.sum(copies_from_all(array, axes).astype(F32), axis=0)


def sent_and_summed(blocks, axes):
    return jnp.sum(lax.all_to_all(blocks, axes, 0, 0, tiled=True).astype(F32), axis=0)


def rows_from(array, start, rows):
    return lax.dynamic_slice(array, (start, jnp.uint32(0)), (rows, array.shape[1]))


def body(trial, screened, val_points, cond_points, eps_val, eps_cond):
    nv, width = trial.shape[1], trial.shape[2]
    n_cols = cond_points.shape[0]
    blocks = lax.axis_size(PLANE)
    half = width // 2

    x_mine = trial[0].T
    offset = (lax.axis_index(ROW) * width).reshape(1)
    mine, energy = start(offset, x_mine, cond_points.T, eps_val, eps_cond)
    piece = lax.convert_element_type(lax.axis_index("yhi") * half, jnp.uint32)
    own = lax.convert_element_type(lax.axis_index(PLANE) * width, jnp.uint32)
    mine, energy, piece, own = lax.optimization_barrier((mine, energy, piece, own))
    two = lax.all_gather(mine, "y2", axis=0, tiled=False)
    everything = copies_from_all(two, NEAR).reshape(blocks * width, n_cols + nv)
    cond_half = everything[:, :n_cols]
    x_half = everything[:, n_cols:]

    def terms_of(x_half):
        mixed_part = jnp.einsum("cv,cn->vn", x_half, cond_half, preferred_element_type=F32)
        both = lax.all_gather(mixed_part.astype(BF16), "core", axis=0, tiled=False)
        folded_part = folded_tile(both, val_points, screened)
        both = lax.all_gather(folded_part, "core", axis=0, tiled=False)
        folded = (both[0].astype(F32) + both[1].astype(F32)).astype(BF16)
        terms = jnp.einsum("cn,vn->cv", cond_half, folded, preferred_element_type=F32)
        return terms.astype(BF16)

    x_piece = rows_from(x_mine, piece, half)
    energy_piece = rows_from(energy, piece, half)
    for _ in range(APPLY - 1):
        terms = terms_of(x_half).reshape(2 * blocks, half, nv)
        rows = sent_and_summed(terms, WIDE)
        x_piece = energy_piece * x_piece + summed_over_copies(rows.astype(BF16), "z")
        x_half = copies_from_all(x_piece.astype(BF16), WIDE).reshape(blocks * width, nv)

    terms = terms_of(x_half).reshape(blocks, 1, width, nv)
    twice = jnp.broadcast_to(terms, (blocks, 2, width, nv)).reshape(2 * blocks, width, nv)
    rows = sent_and_summed(twice, WIDE)
    x_mine = rows_from(x_half, own, width)
    x_mine = energy * x_mine.astype(F32) + summed_over_copies(rows.astype(BF16), "z")
    return x_mine.T[None]


def solution(mesh):
    devices = mesh.devices.reshape(2, 2, 4, 2, 2, 12)
    fine = Mesh(devices, ("y2", "y1", "x", "core", "yhi", "z"))
    in_specs = (P(None, None, ROW), P(ROW, COL), P(ROW, None), P(COL, ROW), P(), P())
    out_specs = P(None, None, ROW)
    return jax.shard_map(body, mesh=fine, in_specs=in_specs, out_specs=out_specs, check_vma=False)
```

```python
import jax
import jax.numpy as jnp
from jax import lax
from jax.experimental import pallas as pl
from jax.experimental.pallas import tpu as pltpu
from jax.sharding import Mesh, PartitionSpec as P

APPLY = 2
F32 = jnp.float32
BF16 = jnp.bfloat16

ROW = ("y2", "y1", "x", "core")
COL = ("yhi", "z3", "za", "zb")
RING = ("zb", "za", "z3")
NEAR = ("y1", "x")
PLANE = ("y1", "x", "y2")
WIDE = ("y1", "x", "y2", "yhi")

VMEM = pl.BlockSpec(memory_space=pltpu.VMEM)


def start_kernel(trial_ref, cond_ref, mine_ref):
    n_cols = cond_ref.shape[1]
    mine_ref[:, :n_cols] = cond_ref[...]
    mine_ref[:, n_cols:] = trial_ref[...].astype(BF16)


def start(trial, cond):
    width, n_cols = cond.shape
    nv = trial.shape[1]
    return pl.pallas_call(
        start_kernel,
        out_shape=jax.ShapeDtypeStruct((width, n_cols + nv), BF16),
        in_specs=[VMEM, VMEM],
        out_specs=VMEM,
        compiler_params=pltpu.CompilerParams(vmem_limit_bytes=1 << 20),
        name="start",
    )(trial, cond)


def energy_kernel(offset_ref, val_ref, levels_ref, energy_ref):
    width = energy_ref.shape[0]
    lanes = levels_ref.shape[1]
    offset = offset_ref[0]
    group = levels_ref[pl.ds(offset // lanes, 1), :]
    lane = lax.broadcasted_iota(jnp.int32, (width, lanes), 1)
    row = lax.broadcasted_iota(jnp.int32, (width, lanes), 0)
    picked = jnp.where(lane == row + offset % lanes, group, 0.0)
    energy_ref[...] = jnp.sum(picked, axis=1, keepdims=True) - val_ref[...]


def energies(offset, width, eps_val, eps_cond):
    nv = eps_val.shape[0]
    lanes = 128
    return pl.pallas_call(
        energy_kernel,
        out_shape=jax.ShapeDtypeStruct((width, nv), F32),
        in_specs=[pl.BlockSpec(memory_space=pltpu.SMEM), VMEM, VMEM],
        out_specs=VMEM,
        compiler_params=pltpu.CompilerParams(vmem_limit_bytes=1 << 20),
        name="energy",
    )(offset, eps_val.reshape(1, nv), eps_cond.reshape(-1, lanes))


def tile_kernel(both_ref, val_ref, screened_ref, out_ref, tile):
    nv = out_ref.shape[0]
    mixed = (both_ref[:nv, :].astype(F32) + both_ref[nv:, :].astype(F32)).astype(BF16)
    inner = jnp.dot(val_ref[...], mixed, preferred_element_type=F32)
    tile[...] = (screened_ref[...].astype(F32) * inner).astype(BF16)
    folded = lax.dot_general(val_ref[...], tile[...], (((0,), (0,)), ((), ())), preferred_element_type=F32)
    out_ref[...] = folded.astype(BF16)


def folded_tile(both, val_points, screened):
    m, nv = val_points.shape
    n = screened.shape[1]
    return pl.pallas_call(
        tile_kernel,
        out_shape=jax.ShapeDtypeStruct((nv, n), BF16),
        in_specs=[VMEM, VMEM, VMEM],
        out_specs=VMEM,
        scratch_shapes=[pltpu.VMEM((m, n), BF16)],
        compiler_params=pltpu.CompilerParams(vmem_limit_bytes=16 << 20),
        cost_estimate=pl.CostEstimate(flops=4 * m * n * nv, bytes_accessed=2 * m * n, transcendentals=0),
        name="tile",
    )(both.reshape(2 * nv, n), val_points, screened)


def copies_from_all(array, axes):
    devices = lax.axis_size(axes)
    copies = jnp.broadcast_to(array, (devices, *array.shape))
    return lax.all_to_all(copies, axes, 0, 0, tiled=True)


def summed_over_copies(array, axes):
    return jnp.sum(copies_from_all(array, axes).astype(F32), axis=0)


def sent_and_summed(blocks, axes):
    return jnp.sum(lax.all_to_all(blocks, axes, 0, 0, tiled=True).astype(F32), axis=0)


def rows_from(array, start, rows):
    return lax.dynamic_slice(array, (start, jnp.uint32(0)), (rows, array.shape[1]))


def body(trial, screened, val_points, cond_points, eps_val, eps_cond):
    nv, width = trial.shape[1], trial.shape[2]
    n_cols = cond_points.shape[0]
    blocks = lax.axis_size(PLANE)
    half = width // 2

    x_mine = trial[0].T
    mine = start(x_mine, cond_points.T)
    offset = (lax.axis_index(ROW) * width).reshape(1)
    piece = lax.convert_element_type(lax.axis_index("yhi") * half, jnp.uint32)
    own = lax.convert_element_type(lax.axis_index(PLANE) * width, jnp.uint32)
    mine, offset, piece, own = lax.optimization_barrier((mine, offset, piece, own))
    two = lax.all_gather(mine, "y2", axis=0, tiled=False)
    everything = copies_from_all(two, NEAR).reshape(blocks * width, n_cols + nv)
    everything, eps_val, eps_cond = lax.optimization_barrier((everything, eps_val, eps_cond))
    energy = energies(offset, width, eps_val, eps_cond)
    cond_half = everything[:, :n_cols]
    x_half = everything[:, n_cols:]

    def terms_of(x_half):
        mixed_part = jnp.einsum("cv,cn->vn", x_half, cond_half, preferred_element_type=F32)
        both = lax.all_gather(mixed_part.astype(BF16), "core", axis=0, tiled=False)
        folded_part = folded_tile(both, val_points, screened)
        both = lax.all_gather(folded_part, "core", axis=0, tiled=False)
        folded = (both[0].astype(F32) + both[1].astype(F32)).astype(BF16)
        terms = jnp.einsum("cn,vn->cv", cond_half, folded, preferred_element_type=F32)
        return terms.astype(BF16)

    x_piece = rows_from(x_mine, piece, half)
    energy_piece = rows_from(energy, piece, half)
    for _ in range(APPLY - 1):
        terms = terms_of(x_half).reshape(2 * blocks, half, nv)
        rows = sent_and_summed(terms, WIDE)
        x_piece = energy_piece * x_piece + summed_over_copies(rows.astype(BF16), RING)
        x_half = copies_from_all(x_piece.astype(BF16), WIDE).reshape(blocks * width, nv)

    terms = terms_of(x_half).reshape(blocks, 1, width, nv)
    twice = jnp.broadcast_to(terms, (blocks, 2, width, nv)).reshape(2 * blocks, width, nv)
    rows = sent_and_summed(twice, WIDE)
    x_mine = rows_from(x_half, own, width)
    x_mine = energy * x_mine.astype(F32) + summed_over_copies(rows.astype(BF16), RING)
    return x_mine.T[None]


def solution(mesh):
    devices = mesh.devices.reshape(2, 2, 4, 2, 2, 3, 2, 2)
    fine = Mesh(devices, ("y2", "y1", "x", "core", "yhi", "z3", "za", "zb"))
    in_specs = (P(None, None, ROW), P(ROW, COL), P(ROW, None), P(COL, ROW), P(), P())
    out_specs = P(None, None, ROW)
    return jax.shard_map(body, mesh=fine, in_specs=in_specs, out_specs=out_specs, check_vma=False)
```

```python
import jax
import jax.numpy as jnp
from jax import lax
from jax.experimental import pallas as pl
from jax.experimental.pallas import tpu as pltpu
from jax.sharding import Mesh, PartitionSpec as P

APPLY = 2
F32 = jnp.float32
BF16 = jnp.bfloat16

ROW = ("y2", "y1", "x", "core")
COL = ("yhi", "z3", "za", "zb")
RING = ("zb", "za", "z3")
NEAR = ("y1", "x")
PLANE = ("y1", "x", "y2")
WIDE = ("y1", "x", "y2", "yhi")

VMEM = pl.BlockSpec(memory_space=pltpu.VMEM)
HBM = pl.BlockSpec(memory_space=pltpu.HBM)


def start_kernel(offset_ref, trial_hbm, cond_hbm, val_hbm, levels_hbm, mine_ref, energy_ref, trial_ref, cond_ref, val_ref, levels_ref, sems):
    width, n_cols = cond_ref.shape
    lanes = levels_ref.shape[1]
    pairs = ((cond_hbm, cond_ref), (trial_hbm, trial_ref), (levels_hbm, levels_ref), (val_hbm, val_ref))
    copies = [pltpu.make_async_copy(*pair, sems.at[k]) for k, pair in enumerate(pairs)]
    for copy in copies:
        copy.start()
    for copy in copies:
        copy.wait()
    mine_ref[:, :n_cols] = cond_ref[...]
    mine_ref[:, n_cols:] = trial_ref[...].astype(BF16)
    offset = offset_ref[0]
    group = levels_ref[pl.ds(offset // lanes, 1), :]
    lane = lax.broadcasted_iota(jnp.int32, (width, lanes), 1)
    row = lax.broadcasted_iota(jnp.int32, (width, lanes), 0)
    picked = jnp.where(lane == row + offset % lanes, group, 0.0)
    energy_ref[...] = jnp.sum(picked, axis=1, keepdims=True) - val_ref[...]


def start(offset, trial, cond, eps_val, eps_cond):
    width, n_cols = cond.shape
    nv = trial.shape[1]
    lanes = 128
    operands = (trial, cond, eps_val.reshape(1, nv), eps_cond.reshape(-1, lanes))
    operands = [pltpu.with_memory_space_constraint(x, pltpu.HBM) for x in operands]
    return pl.pallas_call(
        start_kernel,
        out_shape=(
            pltpu.VMEM((width, n_cols + nv), BF16),
            pltpu.VMEM((width, nv), F32),
        ),
        in_specs=[pl.BlockSpec(memory_space=pltpu.SMEM), HBM, HBM, HBM, HBM],
        out_specs=(VMEM, VMEM),
        scratch_shapes=[pltpu.VMEM(x.shape, x.dtype) for x in operands] + [pltpu.SemaphoreType.DMA((4,))],
        compiler_params=pltpu.CompilerParams(vmem_limit_bytes=1 << 20),
        name="start",
    )(offset, *operands)


def tile_kernel(both_ref, val_ref, screened_ref, out_ref, tile):
    nv = out_ref.shape[0]
    mixed = (both_ref[:nv, :].astype(F32) + both_ref[nv:, :].astype(F32)).astype(BF16)
    inner = jnp.dot(val_ref[...], mixed, preferred_element_type=F32)
    tile[...] = (screened_ref[...].astype(F32) * inner).astype(BF16)
    folded = lax.dot_general(val_ref[...], tile[...], (((0,), (0,)), ((), ())), preferred_element_type=F32)
    out_ref[...] = folded.astype(BF16)


def folded_tile(both, val_points, screened):
    m, nv = val_points.shape
    n = screened.shape[1]
    return pl.pallas_call(
        tile_kernel,
        out_shape=jax.ShapeDtypeStruct((nv, n), BF16),
        in_specs=[VMEM, VMEM, VMEM],
        out_specs=VMEM,
        scratch_shapes=[pltpu.VMEM((m, n), BF16)],
        compiler_params=pltpu.CompilerParams(vmem_limit_bytes=16 << 20),
        cost_estimate=pl.CostEstimate(flops=4 * m * n * nv, bytes_accessed=2 * m * n, transcendentals=0),
        name="tile",
    )(both.reshape(2 * nv, n), val_points, screened)


def copies_from_all(array, axes):
    devices = lax.axis_size(axes)
    copies = jnp.broadcast_to(array, (devices, *array.shape))
    return lax.all_to_all(copies, axes, 0, 0, tiled=True)


def summed_over_copies(array, axes):
    return jnp.sum(copies_from_all(array, axes).astype(F32), axis=0)


def sent_and_summed(blocks, axes):
    return jnp.sum(lax.all_to_all(blocks, axes, 0, 0, tiled=True).astype(F32), axis=0)


def rows_from(array, start, rows):
    return lax.dynamic_slice(array, (start, jnp.uint32(0)), (rows, array.shape[1]))


def body(trial, screened, val_points, cond_points, eps_val, eps_cond):
    nv, width = trial.shape[1], trial.shape[2]
    n_cols = cond_points.shape[0]
    blocks = lax.axis_size(PLANE)
    half = width // 2

    x_mine = trial[0].T
    offset = (lax.axis_index(ROW) * width).reshape(1)
    mine, energy = start(offset, x_mine, cond_points.T, eps_val, eps_cond)
    piece = lax.convert_element_type(lax.axis_index("yhi") * half, jnp.uint32)
    own = lax.convert_element_type(lax.axis_index(PLANE) * width, jnp.uint32)
    mine, energy, piece, own = lax.optimization_barrier((mine, energy, piece, own))
    two = lax.all_gather(mine, "y2", axis=0, tiled=False)
    everything = copies_from_all(two, NEAR).reshape(blocks * width, n_cols + nv)
    cond_half = everything[:, :n_cols]
    x_half = everything[:, n_cols:]

    def terms_of(x_half):
        mixed_part = jnp.einsum("cv,cn->vn", x_half, cond_half, preferred_element_type=F32)
        both = lax.all_gather(mixed_part.astype(BF16), "core", axis=0, tiled=False)
        folded_part = folded_tile(both, val_points, screened)
        both = lax.all_gather(folded_part, "core", axis=0, tiled=False)
        folded = (both[0].astype(F32) + both[1].astype(F32)).astype(BF16)
        terms = jnp.einsum("cn,vn->cv", cond_half, folded, preferred_element_type=F32)
        return terms.astype(BF16)

    x_piece = rows_from(x_mine, piece, half)
    energy_piece = rows_from(energy, piece, half)
    for _ in range(APPLY - 1):
        terms = terms_of(x_half).reshape(2 * blocks, half, nv)
        rows = sent_and_summed(terms, WIDE)
        x_piece = energy_piece * x_piece + summed_over_copies(rows.astype(BF16), RING)
        x_half = copies_from_all(x_piece.astype(BF16), WIDE).reshape(blocks * width, nv)

    terms = terms_of(x_half).reshape(blocks, 1, width, nv)
    twice = jnp.broadcast_to(terms, (blocks, 2, width, nv)).reshape(2 * blocks, width, nv)
    rows = sent_and_summed(twice, WIDE)
    x_mine = rows_from(x_half, own, width)
    x_mine = energy * x_mine.astype(F32) + summed_over_copies(rows.astype(BF16), RING)
    return x_mine.T[None]


def solution(mesh):
    devices = mesh.devices.reshape(2, 2, 4, 2, 2, 3, 2, 2)
    fine = Mesh(devices, ("y2", "y1", "x", "core", "yhi", "z3", "za", "zb"))
    in_specs = (P(None, None, ROW), P(ROW, COL), P(ROW, None), P(COL, ROW), P(), P())
    out_specs = P(None, None, ROW)
    return jax.shard_map(body, mesh=fine, in_specs=in_specs, out_specs=out_specs, check_vma=False)
```

```python
import jax
import jax.numpy as jnp
from jax import lax
from jax.experimental import pallas as pl
from jax.experimental.pallas import tpu as pltpu
from jax.sharding import Mesh, PartitionSpec as P

APPLY = 2
F32 = jnp.float32
BF16 = jnp.bfloat16

ROW = ("y2", "y1", "x", "core")
COL = ("yhi", "z3", "za", "zb")
RING = ("zb", "za", "z3")
NEAR = ("y1", "x")
PLANE = ("y1", "x", "y2")
WIDE = ("y1", "x", "y2", "yhi")

VMEM = pl.BlockSpec(memory_space=pltpu.VMEM)
HBM = pl.BlockSpec(memory_space=pltpu.HBM)


def start_kernel(offset_ref, trial_hbm, cond_hbm, val_hbm, levels_hbm, mine_ref, energy_ref, trial_ref, cond_ref, val_ref, levels_ref, sems):
    width, n_cols = cond_ref.shape
    lanes = levels_ref.shape[1]
    pairs = ((cond_hbm, cond_ref), (trial_hbm, trial_ref), (levels_hbm, levels_ref), (val_hbm, val_ref))
    copies = [pltpu.make_async_copy(*pair, sems.at[k]) for k, pair in enumerate(pairs)]
    for copy in copies:
        copy.start()
    for copy in copies:
        copy.wait()
    mine_ref[:, :n_cols] = cond_ref[...]
    mine_ref[:, n_cols:] = trial_ref[...].astype(BF16)
    offset = offset_ref[0]
    group = levels_ref[pl.ds(offset // lanes, 1), :]
    lane = lax.broadcasted_iota(jnp.int32, (width, lanes), 1)
    row = lax.broadcasted_iota(jnp.int32, (width, lanes), 0)
    picked = jnp.where(lane == row + offset % lanes, group, 0.0)
    energy_ref[...] = jnp.sum(picked, axis=1, keepdims=True) - val_ref[...]


def start(offset, trial, cond, eps_val, eps_cond):
    width, n_cols = cond.shape
    nv = trial.shape[1]
    lanes = 128
    operands = (trial, cond, eps_val.reshape(1, nv), eps_cond.reshape(-1, lanes))
    operands = [pltpu.with_memory_space_constraint(x, pltpu.HBM) for x in operands]
    return pl.pallas_call(
        start_kernel,
        out_shape=(
            pltpu.VMEM((width, n_cols + nv), BF16),
            pltpu.VMEM((width, nv), F32),
        ),
        in_specs=[pl.BlockSpec(memory_space=pltpu.SMEM), HBM, HBM, HBM, HBM],
        out_specs=(VMEM, VMEM),
        scratch_shapes=[pltpu.VMEM(x.shape, x.dtype) for x in operands] + [pltpu.SemaphoreType.DMA((4,))],
        compiler_params=pltpu.CompilerParams(vmem_limit_bytes=1 << 20),
        name="start",
    )(offset, *operands)


def tile_kernel(both_ref, val_ref, screened_ref, out_ref, tile):
    nv = out_ref.shape[0]
    mixed = (both_ref[:nv, :].astype(F32) + both_ref[nv:, :].astype(F32)).astype(BF16)
    inner = jnp.dot(val_ref[...], mixed, preferred_element_type=F32)
    tile[...] = (screened_ref[...].astype(F32) * inner).astype(BF16)
    folded = lax.dot_general(val_ref[...], tile[...], (((0,), (0,)), ((), ())), preferred_element_type=F32)
    out_ref[...] = folded.astype(BF16)


def folded_tile(both, val_points, screened):
    m, nv = val_points.shape
    n = screened.shape[1]
    return pl.pallas_call(
        tile_kernel,
        out_shape=jax.ShapeDtypeStruct((nv, n), BF16),
        in_specs=[VMEM, VMEM, VMEM],
        out_specs=VMEM,
        scratch_shapes=[pltpu.VMEM((m, n), BF16)],
        compiler_params=pltpu.CompilerParams(vmem_limit_bytes=16 << 20),
        cost_estimate=pl.CostEstimate(flops=4 * m * n * nv, bytes_accessed=2 * m * n, transcendentals=0),
        name="tile",
    )(both.reshape(2 * nv, n), val_points, screened)


def copies_from_all(array, axes):
    devices = lax.axis_size(axes)
    copies = jnp.broadcast_to(array, (devices, *array.shape))
    return lax.all_to_all(copies, axes, 0, 0, tiled=True)


def summed_over_copies(array, axes):
    return jnp.sum(copies_from_all(array, axes).astype(F32), axis=0)


def sent_and_summed(blocks, axes):
    return jnp.sum(lax.all_to_all(blocks, axes, 0, 0, tiled=True).astype(F32), axis=0)


def rows_from(array, start, rows):
    return lax.dynamic_slice(array, (start, jnp.uint32(0)), (rows, array.shape[1]))


def body(trial, screened, val_points, cond_points, eps_val, eps_cond):
    nv, width = trial.shape[1], trial.shape[2]
    n_cols = cond_points.shape[0]
    blocks = lax.axis_size(PLANE)
    half = width // 2

    x_mine = trial[0].T
    offset = (lax.axis_index(ROW) * width).reshape(1)
    mine, energy = start(offset, x_mine, cond_points.T, eps_val, eps_cond)
    piece = lax.convert_element_type(lax.axis_index("yhi") * half, jnp.uint32)
    own = lax.convert_element_type(lax.axis_index(PLANE) * width, jnp.uint32)
    mine, energy, piece, own = lax.optimization_barrier((mine, energy, piece, own))
    two = lax.all_gather(mine, "y2", axis=0, tiled=False)
    everything = copies_from_all(two, NEAR).reshape(blocks * width, n_cols + nv)
    cond_half = everything[:, :n_cols]
    x_half = everything[:, n_cols:]

    def terms_of(x_half):
        mixed_part = jnp.einsum("cv,cn->vn", x_half, cond_half, preferred_element_type=F32)
        both = lax.all_gather(mixed_part.astype(BF16), "core", axis=0, tiled=False)
        folded_part = folded_tile(both, val_points, screened)
        both = lax.all_gather(folded_part, "core", axis=0, tiled=False)
        folded = (both[0].astype(F32) + both[1].astype(F32)).astype(BF16)
        terms = jnp.einsum("cn,vn->cv", cond_half, folded, preferred_element_type=F32)
        return terms.astype(BF16)

    x_piece = rows_from(x_mine, piece, half)
    energy_piece = rows_from(energy, piece, half)
    for _ in range(APPLY - 1):
        terms = terms_of(x_half).reshape(2 * blocks, half, nv)
        rows = sent_and_summed(terms, WIDE)
        x_piece = energy_piece * x_piece + summed_over_copies(rows.astype(BF16), RING)
        x_half = copies_from_all(x_piece.astype(BF16), WIDE).reshape(blocks * width, nv)

    terms = terms_of(x_half).reshape(blocks, width, nv)
    rows = sent_and_summed(terms, PLANE)
    x_mine = rows_from(x_half, own, width)
    along = summed_over_copies(rows.astype(BF16), RING).astype(BF16)
    both = lax.all_gather(along, "yhi", axis=0, tiled=False)
    x_mine = energy * x_mine.astype(F32) + (both[0].astype(F32) + both[1].astype(F32))
    return x_mine.T[None]


def solution(mesh):
    devices = mesh.devices.reshape(2, 2, 4, 2, 2, 3, 2, 2)
    fine = Mesh(devices, ("y2", "y1", "x", "core", "yhi", "z3", "za", "zb"))
    in_specs = (P(None, None, ROW), P(ROW, COL), P(ROW, None), P(COL, ROW), P(), P())
    out_specs = P(None, None, ROW)
    return jax.shard_map(body, mesh=fine, in_specs=in_specs, out_specs=out_specs, check_vma=False)
```

```python
import jax
import jax.numpy as jnp
from jax import lax
from jax.experimental import pallas as pl
from jax.experimental.pallas import tpu as pltpu
from jax.sharding import Mesh, PartitionSpec as P

APPLY = 2
F32 = jnp.float32
BF16 = jnp.bfloat16

ROW = ("y2", "y1", "x", "core")
COL = ("yhi", "z3", "za", "zb")
RING = ("zb", "za", "z3")
NEAR = ("y1", "x")
PLANE = ("y1", "x", "y2")
WIDE = ("y1", "x", "y2", "yhi")

VMEM = pl.BlockSpec(memory_space=pltpu.VMEM)
HBM = pl.BlockSpec(memory_space=pltpu.HBM)


def start_kernel(offset_ref, trial_hbm, cond_hbm, val_hbm, levels_hbm, mine_ref, energy_ref, trial_ref, cond_ref, val_ref, levels_ref, sems):
    width, n_cols = cond_ref.shape
    lanes = levels_ref.shape[1]
    pairs = ((cond_hbm, cond_ref), (trial_hbm, trial_ref), (levels_hbm, levels_ref), (val_hbm, val_ref))
    copies = [pltpu.make_async_copy(*pair, sems.at[k]) for k, pair in enumerate(pairs)]
    for copy in copies:
        copy.start()
    for copy in copies[1:]:
        copy.wait()
    mine_ref[:, n_cols:] = trial_ref[...].astype(BF16)
    offset = offset_ref[0]
    group = levels_ref[pl.ds(offset // lanes, 1), :]
    lane = lax.broadcasted_iota(jnp.int32, (width, lanes), 1)
    row = lax.broadcasted_iota(jnp.int32, (width, lanes), 0)
    picked = jnp.where(lane == row + offset % lanes, group, 0.0)
    energy_ref[...] = jnp.sum(picked, axis=1, keepdims=True) - val_ref[...]
    copies[0].wait()
    mine_ref[:, :n_cols] = cond_ref[...]


def start(offset, trial, cond, eps_val, eps_cond):
    width, n_cols = cond.shape
    nv = trial.shape[1]
    lanes = 128
    operands = (trial, cond, eps_val.reshape(1, nv), eps_cond.reshape(-1, lanes))
    operands = [pltpu.with_memory_space_constraint(x, pltpu.HBM) for x in operands]
    return pl.pallas_call(
        start_kernel,
        out_shape=(
            pltpu.VMEM((width, n_cols + nv), BF16),
            pltpu.VMEM((width, nv), F32),
        ),
        in_specs=[pl.BlockSpec(memory_space=pltpu.SMEM), HBM, HBM, HBM, HBM],
        out_specs=(VMEM, VMEM),
        scratch_shapes=[pltpu.VMEM(x.shape, x.dtype) for x in operands] + [pltpu.SemaphoreType.DMA((4,))],
        compiler_params=pltpu.CompilerParams(vmem_limit_bytes=1 << 20),
        name="start",
    )(offset, *operands)


def tile_kernel(both_ref, val_ref, screened_ref, out_ref, tile):
    nv = out_ref.shape[0]
    mixed = (both_ref[:nv, :].astype(F32) + both_ref[nv:, :].astype(F32)).astype(BF16)
    inner = jnp.dot(val_ref[...], mixed, preferred_element_type=F32)
    tile[...] = (screened_ref[...].astype(F32) * inner).astype(BF16)
    folded = lax.dot_general(val_ref[...], tile[...], (((0,), (0,)), ((), ())), preferred_element_type=F32)
    out_ref[...] = folded.astype(BF16)


def folded_tile(both, val_points, screened):
    m, nv = val_points.shape
    n = screened.shape[1]
    return pl.pallas_call(
        tile_kernel,
        out_shape=jax.ShapeDtypeStruct((nv, n), BF16),
        in_specs=[VMEM, VMEM, VMEM],
        out_specs=VMEM,
        scratch_shapes=[pltpu.VMEM((m, n), BF16)],
        compiler_params=pltpu.CompilerParams(vmem_limit_bytes=16 << 20),
        cost_estimate=pl.CostEstimate(flops=4 * m * n * nv, bytes_accessed=2 * m * n, transcendentals=0),
        name="tile",
    )(both.reshape(2 * nv, n), val_points, screened)


def copies_from_all(array, axes):
    devices = lax.axis_size(axes)
    copies = jnp.broadcast_to(array, (devices, *array.shape))
    return lax.all_to_all(copies, axes, 0, 0, tiled=True)


def summed_over_copies(array, axes):
    return jnp.sum(copies_from_all(array, axes).astype(F32), axis=0)


def sent_and_summed(blocks, axes):
    return jnp.sum(lax.all_to_all(blocks, axes, 0, 0, tiled=True).astype(F32), axis=0)


def rows_from(array, start, rows):
    return lax.dynamic_slice(array, (start, jnp.uint32(0)), (rows, array.shape[1]))


def body(trial, screened, val_points, cond_points, eps_val, eps_cond):
    nv, width = trial.shape[1], trial.shape[2]
    n_cols = cond_points.shape[0]
    blocks = lax.axis_size(PLANE)
    half = width // 2

    x_mine = trial[0].T
    offset = (lax.axis_index(ROW) * width).reshape(1)
    mine, energy = start(offset, x_mine, cond_points.T, eps_val, eps_cond)
    piece = lax.convert_element_type(lax.axis_index("yhi") * half, jnp.uint32)
    own = lax.convert_element_type(lax.axis_index(PLANE) * width, jnp.uint32)
    mine, energy, piece, own = lax.optimization_barrier((mine, energy, piece, own))
    two = lax.all_gather(mine, "y2", axis=0, tiled=False)
    everything = copies_from_all(two, NEAR).reshape(blocks * width, n_cols + nv)
    cond_half = everything[:, :n_cols]
    x_half = everything[:, n_cols:]

    def terms_of(x_half):
        mixed_part = jnp.einsum("cv,cn->vn", x_half, cond_half, preferred_element_type=F32)
        both = lax.all_gather(mixed_part.astype(BF16), "core", axis=0, tiled=False)
        folded_part = folded_tile(both, val_points, screened)
        both = lax.all_gather(folded_part, "core", axis=0, tiled=False)
        folded = (both[0].astype(F32) + both[1].astype(F32)).astype(BF16)
        terms = jnp.einsum("cn,vn->cv", cond_half, folded, preferred_element_type=F32)
        return terms.astype(BF16)

    x_piece = rows_from(x_mine, piece, half)
    energy_piece = rows_from(energy, piece, half)
    for _ in range(APPLY - 1):
        terms = terms_of(x_half).reshape(2 * blocks, half, nv)
        rows = sent_and_summed(terms, WIDE)
        x_piece = energy_piece * x_piece + summed_over_copies(rows.astype(BF16), RING)
        x_half = copies_from_all(x_piece.astype(BF16), WIDE).reshape(blocks * width, nv)

    terms = terms_of(x_half).reshape(blocks, width, nv)
    rows = sent_and_summed(terms, PLANE)
    x_mine = rows_from(x_half, own, width)
    both = lax.all_gather(rows.astype(BF16), "yhi", axis=0, tiled=False)
    rows = both[0].astype(F32) + both[1].astype(F32)
    x_mine = energy * x_mine.astype(F32) + summed_over_copies(rows.astype(BF16), RING)
    return x_mine.T[None]


def solution(mesh):
    devices = mesh.devices.reshape(2, 2, 4, 2, 2, 3, 2, 2)
    fine = Mesh(devices, ("y2", "y1", "x", "core", "yhi", "z3", "za", "zb"))
    in_specs = (P(None, None, ROW), P(ROW, COL), P(ROW, None), P(COL, ROW), P(), P())
    out_specs = P(None, None, ROW)
    return jax.shard_map(body, mesh=fine, in_specs=in_specs, out_specs=out_specs, check_vma=False)
```

```python
import jax
import jax.numpy as jnp
from jax import lax
from jax.experimental import pallas as pl
from jax.experimental.pallas import tpu as pltpu
from jax.sharding import Mesh, PartitionSpec as P

APPLY = 2
F32 = jnp.float32
BF16 = jnp.bfloat16

ROW = ("y2", "y1", "x", "core")
COL = ("yhi", "z3", "za", "zb")
RING = ("zb", "z3", "za")
NEAR = ("y1", "x")
PLANE = ("y1", "x", "y2")
WIDE = ("y1", "x", "y2", "yhi")

VMEM = pl.BlockSpec(memory_space=pltpu.VMEM)
HBM = pl.BlockSpec(memory_space=pltpu.HBM)


def start_kernel(offset_ref, trial_hbm, cond_hbm, val_hbm, levels_hbm, mine_ref, energy_ref, trial_ref, cond_ref, val_ref, levels_ref, sems):
    width, n_cols = cond_ref.shape
    lanes = levels_ref.shape[1]
    pairs = ((cond_hbm, cond_ref), (trial_hbm, trial_ref), (levels_hbm, levels_ref), (val_hbm, val_ref))
    copies = [pltpu.make_async_copy(*pair, sems.at[k]) for k, pair in enumerate(pairs)]
    for copy in copies:
        copy.start()
    for copy in copies:
        copy.wait()
    mine_ref[:, :n_cols] = cond_ref[...]
    mine_ref[:, n_cols:] = trial_ref[...].astype(BF16)
    offset = offset_ref[0]
    group = levels_ref[pl.ds(offset // lanes, 1), :]
    lane = lax.broadcasted_iota(jnp.int32, (width, lanes), 1)
    row = lax.broadcasted_iota(jnp.int32, (width, lanes), 0)
    picked = jnp.where(lane == row + offset % lanes, group, 0.0)
    energy_ref[...] = jnp.sum(picked, axis=1, keepdims=True) - val_ref[...]


def start(offset, trial, cond, eps_val, eps_cond):
    width, n_cols = cond.shape
    nv = trial.shape[1]
    lanes = 128
    operands = (trial, cond, eps_val.reshape(1, nv), eps_cond.reshape(-1, lanes))
    operands = [pltpu.with_memory_space_constraint(x, pltpu.HBM) for x in operands]
    return pl.pallas_call(
        start_kernel,
        out_shape=(
            pltpu.VMEM((width, n_cols + nv), BF16),
            pltpu.VMEM((width, nv), F32),
        ),
        in_specs=[pl.BlockSpec(memory_space=pltpu.SMEM), HBM, HBM, HBM, HBM],
        out_specs=(VMEM, VMEM),
        scratch_shapes=[pltpu.VMEM(x.shape, x.dtype) for x in operands] + [pltpu.SemaphoreType.DMA((4,))],
        compiler_params=pltpu.CompilerParams(vmem_limit_bytes=1 << 20),
        name="start",
    )(offset, *operands)


def tile_kernel(both_ref, val_ref, screened_ref, out_ref, tile):
    nv = out_ref.shape[0]
    mixed = (both_ref[:nv, :].astype(F32) + both_ref[nv:, :].astype(F32)).astype(BF16)
    inner = jnp.dot(val_ref[...], mixed, preferred_element_type=F32)
    tile[...] = (screened_ref[...].astype(F32) * inner).astype(BF16)
    folded = lax.dot_general(val_ref[...], tile[...], (((0,), (0,)), ((), ())), preferred_element_type=F32)
    out_ref[...] = folded.astype(BF16)


def folded_tile(both, val_points, screened):
    m, nv = val_points.shape
    n = screened.shape[1]
    return pl.pallas_call(
        tile_kernel,
        out_shape=jax.ShapeDtypeStruct((nv, n), BF16),
        in_specs=[VMEM, VMEM, VMEM],
        out_specs=VMEM,
        scratch_shapes=[pltpu.VMEM((m, n), BF16)],
        compiler_params=pltpu.CompilerParams(vmem_limit_bytes=16 << 20),
        cost_estimate=pl.CostEstimate(flops=4 * m * n * nv, bytes_accessed=2 * m * n, transcendentals=0),
        name="tile",
    )(both.reshape(2 * nv, n), val_points, screened)


def copies_from_all(array, axes):
    devices = lax.axis_size(axes)
    copies = jnp.broadcast_to(array, (devices, *array.shape))
    return lax.all_to_all(copies, axes, 0, 0, tiled=True)


def summed_over_copies(array, axes):
    return jnp.sum(copies_from_all(array, axes).astype(F32), axis=0)


def sent_and_summed(blocks, axes):
    return jnp.sum(lax.all_to_all(blocks, axes, 0, 0, tiled=True).astype(F32), axis=0)


def rows_from(array, start, rows):
    return lax.dynamic_slice(array, (start, jnp.uint32(0)), (rows, array.shape[1]))


def body(trial, screened, val_points, cond_points, eps_val, eps_cond):
    nv, width = trial.shape[1], trial.shape[2]
    n_cols = cond_points.shape[0]
    blocks = lax.axis_size(PLANE)
    half = width // 2

    x_mine = trial[0].T
    offset = (lax.axis_index(ROW) * width).reshape(1)
    mine, energy = start(offset, x_mine, cond_points.T, eps_val, eps_cond)
    piece = lax.convert_element_type(lax.axis_index("yhi") * half, jnp.uint32)
    own = lax.convert_element_type(lax.axis_index(PLANE) * width, jnp.uint32)
    mine, energy, piece, own = lax.optimization_barrier((mine, energy, piece, own))
    two = lax.all_gather(mine, "y2", axis=0, tiled=False)
    everything = copies_from_all(two, NEAR).reshape(blocks * width, n_cols + nv)
    cond_half = everything[:, :n_cols]
    x_half = everything[:, n_cols:]

    def terms_of(x_half):
        mixed_part = jnp.einsum("cv,cn->vn", x_half, cond_half, preferred_element_type=F32)
        both = lax.all_gather(mixed_part.astype(BF16), "core", axis=0, tiled=False)
        folded_part = folded_tile(both, val_points, screened)
        both = lax.all_gather(folded_part, "core", axis=0, tiled=False)
        folded = (both[0].astype(F32) + both[1].astype(F32)).astype(BF16)
        terms = jnp.einsum("cn,vn->cv", cond_half, folded, preferred_element_type=F32)
        return terms.astype(BF16)

    x_piece = rows_from(x_mine, piece, half)
    energy_piece = rows_from(energy, piece, half)
    for _ in range(APPLY - 1):
        terms = terms_of(x_half).reshape(2 * blocks, half, nv)
        rows = sent_and_summed(terms, WIDE)
        x_piece = energy_piece * x_piece + summed_over_copies(rows.astype(BF16), RING)
        x_half = copies_from_all(x_piece.astype(BF16), WIDE).reshape(blocks * width, nv)

    terms = terms_of(x_half).reshape(blocks, width, nv)
    rows = sent_and_summed(terms, PLANE)
    x_mine = rows_from(x_half, own, width)
    along = summed_over_copies(rows.astype(BF16), RING).astype(BF16)
    both = lax.all_gather(along, "yhi", axis=0, tiled=False)
    x_mine = energy * x_mine.astype(F32) + (both[0].astype(F32) + both[1].astype(F32))
    return x_mine.T[None]


def solution(mesh):
    devices = mesh.devices.reshape(2, 2, 4, 2, 2, 3, 2, 2)
    fine = Mesh(devices, ("y2", "y1", "x", "core", "yhi", "z3", "za", "zb"))
    in_specs = (P(None, None, ROW), P(ROW, COL), P(ROW, None), P(COL, ROW), P(), P())
    out_specs = P(None, None, ROW)
    return jax.shard_map(body, mesh=fine, in_specs=in_specs, out_specs=out_specs, check_vma=False)
```
